512 devices in a mesh: seq: 64 (over z_lo, x, y), tp: 8 (over z_hi, core).
Axes of the slice: x: 4, y: 8, z: 8 (z_hi: 4, z_lo: 2; z = z_hi * 2 + z_lo), core: 2. Of those that a mesh axis runs over, the one named last changes fastest.
Arguments:
- patches: bfloat16 [1664, 65536], P('tp', 'seq'), may hold values from -400 to 400
- ln_gain: bfloat16 [1664], P('tp'), may hold values from 0.099609375 to 1.8984375
- ln_bias: bfloat16 [1664], P('tp'), may hold values from -3 to 3
- merge_weight: bfloat16 [4, 1664, 1664], P(None, 'tp', 'seq'), may hold values from -0.078125 to 0.078125
- merge_bias: bfloat16 [1664], P('tp'), may hold values from -3 to 3
- targets: int32 [16384], P('seq'), may hold values from 0 to 24575, as said below
- text_embed: bfloat16 [1664, 24576], P('tp', 'seq'), may hold values from -6 to 6
Outputs:
- prompt_embeds: bfloat16 [1664, 24576], P('tp', 'seq')
The draws below stay inside these ranges and needn't reach their ends.
Inputs may be any that keep to these rules, and one draw needn't show every extreme that they name: `targets`: Distinct. The merged rows of one index of seq go to the positions of 32 indices of seq (position p belongs to index p // 384); at most 10 of them to one index, and exactly 10 to some index, from every index.
All inputs are finite; a program needn't handle non-finite values.
Results may differ from the reference program's by a relative error of at most 0.015.
Values may be sent and summed in bfloat16 or wider, within the bound.
No kernel may reach another device: no remote copies, remote signals or barrier semaphores. Data moves between devices by JAX's collectives and lax.ppermute only.
A program may use at most 64 MiB of HBM per device.

```python
import math
import jax
import jax.numpy as jnp
from jax import lax

D = 1664
GROUP = 4
TOK_DEV = 1024
MERGED_DEV = 256
PROMPT_DEV = 384
CAP = 10
TOKENS = 65536
MERGED = 16384
PROMPTS = 24576
N_SEQ = 64
N_TP = 8


def draw_patches(key, part):
    key_base, key_cols, key_rows = jax.random.split(key, 3)
    col_scale = jnp.exp(jax.random.uniform(key_cols, (D, 1), jnp.float32) * math.log(10.0))
    row_scale = jnp.exp(jax.random.uniform(key_rows, (1, TOKENS), jnp.float32) * math.log(10.0))
    base_vals = jnp.clip(jax.random.normal(key_base, (D, TOKENS), jnp.float32), -3.0, 3.0)
    values = base_vals * col_scale * row_scale
    return values.astype(jnp.bfloat16)


def draw_targets(key, part):
    devices = N_SEQ
    half_count = devices // 2
    mean_rows = 2 * MERGED_DEV // devices
    spread_rows = mean_rows // 4
    key_offs, key_extra, key_slots, key_order = jax.random.split(key, 4)
    key_pick, key_mix = jax.random.split(key_offs, 2)
    others = jax.random.permutation(key_pick, devices - 1).astype(jnp.int32)
    others = others + (others >= half_count).astype(jnp.int32)
    chosen = jnp.concatenate([jnp.full((1,), half_count, jnp.int32), others[:half_count - 1]])
    offsets = chosen[jax.random.permutation(key_mix, half_count)]
    extra_rows = jax.random.randint(key_extra, (devices, half_count // 2), 0, spread_rows + 1)
    extra_rows = extra_rows.at[:, 0].set(spread_rows)
    row_counts = mean_rows + jnp.concatenate([extra_rows, -extra_rows], axis=1)
    group_ends = jnp.cumsum(row_counts, axis=1)
    group_starts = group_ends - row_counts
    indices = jnp.arange(MERGED_DEV, dtype=jnp.int32)
    group_of = jnp.sum((indices[None, :, None] >= group_ends[:, None, :]).astype(jnp.int32), axis=2)
    start_of = jnp.take_along_axis(group_starts, group_of, axis=1)
    within_group = indices[None, :] - start_of
    source_dev = jnp.arange(devices, dtype=jnp.int32)[:, None]
    target_dev = (source_dev + offsets[group_of]) % devices
    slot_table = jax.vmap(lambda key_item: jax.random.permutation(key_item, PROMPT_DEV))(jax.random.split(key_slots, devices))
    local_pos = slot_table[target_dev, group_of * CAP + within_group]
    global_pos = target_dev * PROMPT_DEV + local_pos
    row_order = jax.vmap(lambda key_item: jax.random.permutation(key_item, MERGED_DEV))(jax.random.split(key_order, devices))
    shuffled = jnp.take_along_axis(global_pos, row_order, axis=1)
    return shuffled.reshape(-1).astype(jnp.int32)


def block_scale(rng, shape, cuts, low, high):
    loudness, own = 1.0, jax.random.fold_in(rng, 6)
    for axis_at, blocks in cuts:
        heights = jnp.exp(jax.random.uniform(jax.random.fold_in(own, axis_at), (blocks,), jnp.float32, low / len(cuts), high / len(cuts)))
        loudness = loudness * jnp.repeat(heights, shape[axis_at] // blocks).reshape([-1 if axis == axis_at else 1 for axis in range(len(shape))])
    return loudness


def bell_draw(rng, shape, width, most, pieces=(), held_as=jnp.bfloat16):
    factor_of = block_scale(rng, shape, pieces, -0.22, 0.18) if pieces else 1.0
    result = jax.random.normal(rng, shape, jnp.float32) * width * factor_of
    return jnp.minimum(jnp.maximum(result, -most), most).astype(held_as)


def setup_inputs(seed: int = 0) -> dict:
    key_list = jax.random.split(jax.random.key(seed), 8)
    return {
        "patches": draw_patches(jax.random.fold_in(key_list[7], 71), 0),
        "ln_gain": jnp.clip(1.0 + 0.18 * jax.random.normal(key_list[1], (D,), jnp.float32), 0.099609375, 1.8984375).astype(jnp.bfloat16),
        "ln_bias": bell_draw(key_list[2], (D,), 0.5, 3.0, ((0, 8),)),
        "merge_weight": bell_draw(key_list[3], (GROUP, D, D), (GROUP * D) ** -0.5, 0.078125, ((1, 8), (2, 64))),
        "merge_bias": bell_draw(key_list[4], (D,), 0.5, 3.0, ((0, 8),)),
        "targets": draw_targets(jax.random.fold_in(key_list[7], 71), 0),
        "text_embed": bell_draw(key_list[6], (D, PROMPTS), 1.0, 6.0, ((0, 8), (1, 64))),
    }


def normalize_block(row_block, gain_row, bias_row):
    values = row_block.astype(jnp.float32)
    row_mean = lax.optimization_barrier(jnp.mean(values, axis=1, keepdims=True))
    centered = values - row_mean
    row_var = lax.optimization_barrier(jnp.mean(centered * centered, axis=1, keepdims=True))
    scaled = centered * lax.rsqrt(row_var + 1e-06) * gain_row + bias_row
    return scaled.astype(jnp.bfloat16)

def reference(patches, ln_gain, ln_bias, merge_weight, merge_bias, targets, text_embed):
    gain_row = ln_gain.astype(jnp.float32)
    bias_row = ln_bias.astype(jnp.float32)
    blocks = patches.T.reshape(N_SEQ, TOK_DEV, D)
    normed = lax.map(lambda row_block: normalize_block(row_block, gain_row, bias_row), blocks)
    grouped = normed.reshape(MERGED, GROUP, D)
    group_width = D // N_TP

    def add_group(step_idx, sum_total):
        first = (jnp.asarray(step_idx) * group_width).astype(jnp.int32)
        inputs = lax.dynamic_slice_in_dim(grouped, first, group_width, 2).reshape(MERGED, GROUP * group_width)
        weights = lax.dynamic_slice_in_dim(merge_weight, first, group_width, 1).reshape(GROUP * group_width, D)
        partial_g = lax.optimization_barrier(jnp.dot(inputs, weights, preferred_element_type=jnp.float32).astype(jnp.bfloat16))
        return sum_total + partial_g.astype(jnp.float32)
    sum_total = lax.fori_loop(0, N_TP, add_group, jnp.zeros((MERGED, D), jnp.float32))
    merged = (sum_total + merge_bias.astype(jnp.float32)).astype(jnp.bfloat16)
    return text_embed.at[:, targets].set(merged.T)
```

```python
import functools

import jax
import jax.numpy as jnp
import numpy as np
from jax import lax
from jax.experimental import pallas as pl
from jax.experimental.pallas import tpu as pltpu
from jax.sharding import Mesh
from jax.sharding import PartitionSpec as P

D = 1664
GROUP = 4
N_SEQ = 64
N_TP = 8
FEAT = D // N_TP
TOK = 1024
ROWS = TOK // GROUP
CHUNK = D // N_SEQ
CHUNK_PAD = 32
POS = 384
CAP = 10
SLOTS = 24
HALF = FEAT // 2
LANES = 128
SHARE = ("zl", "xl")
GATHER = ("xh", "y")
SEQ = ("zl", "xh", "xl", "y")
TP = ("zh", "c")
BF16 = jnp.bfloat16
F32 = jnp.float32


def _vmem(n):
    return [pl.BlockSpec(memory_space=pltpu.VMEM)] * n


def _call(body, outs, n_in, n_smem=0):
    return pl.pallas_call(
        body,
        out_shape=outs,
        in_specs=[pl.BlockSpec(memory_space=pltpu.SMEM)] * n_smem + _vmem(n_in),
        out_specs=jax.tree.map(lambda _: pl.BlockSpec(memory_space=pltpu.VMEM), outs),
        compiler_params=pltpu.CompilerParams(vmem_limit_bytes=48 << 20),
    )


def split_body(x_ref, xd_ref, st_ref):
    row = lax.broadcasted_iota(jnp.int32, (512, 512), 0)
    col = lax.broadcasted_iota(jnp.int32, (512, 512), 1)
    pick = jnp.where(row == 4 * (col & 127) + (col >> 7), 1.0, 0.0).astype(BF16)
    for half in range(2):
        lanes = pl.ds(half * 128, 128)
        moved = jnp.dot(x_ref[:, pl.ds(half * 512, 512)], pick, preferred_element_type=F32)
        for k in range(GROUP):
            block = moved[:, k * 128 : (k + 1) * 128]
            xd_ref[pl.ds(k * FEAT, FEAT), lanes] = block.astype(BF16)
            mean = jnp.sum(block, axis=0, keepdims=True) * (1.0 / FEAT)
            off = block - mean
            st_ref[pl.ds(k, 1), lanes] = mean
            st_ref[pl.ds(GROUP + k, 1), lanes] = jnp.sum(off * off, axis=0, keepdims=True)


def project_body(
    ids, own, rx, rk, rs, st, gain, bias, wg, pack, keep_ref, send_ref, normed, weight
):
    c, q = ids[0], ids[1]
    for g in range(2):
        rows = jnp.concatenate([wg[g * 8 + y] for y in range(8)], axis=0)
        weight[g] = jnp.dot(pack[...], rows, preferred_element_type=F32).astype(BF16)
    gain_col = jnp.broadcast_to(gain[...], (FEAT, ROWS))
    bias_col = jnp.broadcast_to(bias[...], (FEAT, ROWS))
    for job in range(4):
        kept, i = job // 2 == 1, job % 2
        e = 2 * (c if kept else 1 - c) + i
        parts = st[q ^ e]
        mean = jnp.sum(parts[:, :GROUP], axis=0) * (1.0 / N_TP)
        off = parts[:, :GROUP] - mean[None]
        var = (jnp.sum(parts[:, GROUP:], axis=0) + FEAT * jnp.sum(off * off, axis=0)) * (1.0 / D)
        scale = lax.rsqrt(var + 1e-06)
        for k in range(GROUP):
            at = pl.ds(k * FEAT, FEAT)
            if i == 1:
                x = (rk if kept else rs)[at, :]
            else:
                x = jnp.where((c == 1) == kept, rx[at, :], own[at, :])
            centered = x.astype(F32) - mean[k : k + 1]
            normed[at, :] = (centered * scale[k : k + 1] * gain_col + bias_col).astype(BF16)
        for g in range(2):
            out = jnp.dot(weight[g], normed[...], preferred_element_type=F32).astype(BF16)
            (keep_ref if kept else send_ref)[2 * i + g] = out


def pair_body(ids, keep, got, *outs):
    zh = ids[0]
    for k in range(4):
        p = zh ^ k
        outs[k][...] = (keep[p].astype(F32) + got[p].astype(F32)).astype(BF16)


def place_body(z0, z1, z2, z3, bias, slot, extra, send_ref):
    total = (z0[...].astype(F32) + z1[...].astype(F32)) + (z2[...].astype(F32) + z3[...].astype(F32))
    merged = total + bias[...]
    fill = jnp.zeros((LANES - HALF - 8, ROWS), F32)
    row = lax.broadcasted_iota(jnp.int32, (N_SEQ * SLOTS, ROWS), 0)
    tag_row = lax.broadcasted_iota(jnp.int32, (8, ROWS), 0)
    out = None
    for h in range(2):
        tag = jnp.where(tag_row == 3, float(h), extra[...])
        data = jnp.concatenate([merged[h * HALF : (h + 1) * HALF], tag, fill], axis=0)
        pick = jnp.where(row == slot[...] + h * CAP, 1.0, 0.0).astype(BF16)
        part = lax.dot_general(
            pick, data.astype(BF16), (((1,), (1,)), ((), ())), preferred_element_type=F32
        )
        out = part if out is None else out + part
    send_ref[...] = out.astype(BF16).reshape(N_SEQ, SLOTS, LANES)


def final_body(got, text, out_ref):
    rows = got[...].reshape(N_SEQ * SLOTS, LANES)
    tags = rows.astype(F32)
    at = tags[:, HALF : HALF + 1] * 16.0 + tags[:, HALF + 1 : HALF + 2] - 16.0
    side = tags[:, HALF + 3 : HALF + 4]
    want = lax.broadcasted_iota(jnp.int32, (N_SEQ * SLOTS, POS), 1).astype(F32)
    halves = []
    for h in range(2):
        mine = jnp.where(side == float(h), at, -1.0)
        pick = jnp.where(want == mine, 1.0, 0.0).astype(BF16)
        halves.append(
            lax.dot_general(rows, pick, (((0,), (0,)), ((), ())), preferred_element_type=F32)
        )
    hit = halves[0][HALF + 2 : HALF + 3] > 0.5
    full = jnp.concatenate([halves[0][:HALF], halves[1][:HALF]], axis=0)
    out_ref[...] = jnp.where(hit, full, text[...].astype(F32)).astype(BF16)


def _pairs(sizes, dest):
    return [
        (int(np.ravel_multi_index(at, sizes)), int(np.ravel_multi_index(dest(*at), sizes)))
        for at in np.ndindex(*sizes)
    ]


def shards(patches, ln_gain, ln_bias, merge_weight, merge_bias, targets, text_embed):
    sds = jax.ShapeDtypeStruct
    zl, xl, zh, c = (lax.axis_index(a) for a in ("zl", "xl", "zh", "c"))

    chunk = jnp.transpose(merge_weight, (2, 0, 1)).reshape(CHUNK, GROUP * FEAT)
    chunk = jnp.pad(chunk, ((0, CHUNK_PAD - CHUNK), (0, 0)))
    columns = lax.all_to_all(
        jnp.broadcast_to(chunk[None], (16, CHUNK_PAD, GROUP * FEAT)), GATHER, 0, 0, tiled=True
    )

    own, stats = _call(split_body, (sds((GROUP * FEAT, ROWS), BF16), sds((8, ROWS), F32)), 1)(patches)
    axes, sizes = ("zl", "xl", "c"), (2, 2, 2)
    rx = lax.ppermute(own, axes, _pairs(sizes, lambda z, x, k: (z ^ 1, x, k)))
    rk = lax.ppermute(own, axes, _pairs(sizes, lambda z, x, k: (z ^ k, x ^ 1, k)))
    rs = lax.ppermute(own, axes, _pairs(sizes, lambda z, x, k: (z ^ k ^ 1, x ^ 1, k)))
    all_stats = lax.all_to_all(
        jnp.broadcast_to(stats[None], (32, 8, ROWS)), SHARE + TP, 0, 0, tiled=True
    ).reshape(4, N_TP, 8, ROWS)

    packed = np.arange(FEAT)
    pack = np.zeros((FEAT, 8 * CHUNK_PAD), np.float32)
    pack[packed, packed // CHUNK * CHUNK_PAD + packed % CHUNK] = 1.0
    ids = jnp.stack([c, 2 * zl + xl]).astype(jnp.int32)
    piece = sds((4, FEAT, ROWS), BF16)
    keep, send = pl.pallas_call(
        project_body,
        out_shape=(piece, piece),
        in_specs=[pl.BlockSpec(memory_space=pltpu.SMEM)] + _vmem(9),
        out_specs=tuple(_vmem(2)),
        scratch_shapes=[
            pltpu.VMEM((GROUP * FEAT, ROWS), BF16),
            pltpu.VMEM((2, FEAT, GROUP * FEAT), BF16),
        ],
        compiler_params=pltpu.CompilerParams(vmem_limit_bytes=48 << 20),
    )(
        ids, own, rx, rk, rs, all_stats,
        ln_gain.astype(F32)[:, None], ln_bias.astype(F32)[:, None], columns, jnp.asarray(pack, BF16),
    )

    got = lax.ppermute(send, "c", [(0, 1), (1, 0)])
    part = sds((FEAT, ROWS), BF16)
    parts = _call(pair_body, (part,) * 4, 2, 1)(zh[None].astype(jnp.int32), keep, got)
    axes, sizes = ("zl", "xl", "zh", "c"), (2, 2, 4, 2)
    moved = [
        lax.ppermute(
            parts[k],
            axes,
            _pairs(sizes, lambda z, x, h, k2, k=k: (z ^ k2, x ^ ((h ^ k) >> 1), 2 * z + ((h ^ k) & 1), x)),
        )
        for k in range(4)
    ]

    target_dev = targets // POS
    local_pos = targets % POS
    before = jnp.arange(ROWS)[:, None] < jnp.arange(ROWS)[None, :]
    rank = jnp.sum(((target_dev[:, None] == target_dev[None, :]) & before).astype(jnp.int32), axis=0)
    slot = (target_dev * SLOTS + rank)[None, :]
    zero = jnp.zeros((ROWS,), F32)
    one = jnp.ones((ROWS,), F32)
    tags = [(local_pos // 16 + 1).astype(F32), (local_pos % 16).astype(F32), one, zero, zero, zero, zero, zero]
    extra = jnp.stack(tags)

    sent = _call(place_body, sds((N_SEQ, SLOTS, LANES), BF16), 7)(
        *moved, merge_bias.astype(F32)[:, None], slot, extra
    )
    rows = lax.all_to_all(sent, SEQ, 0, 0, tiled=True)
    return _call(final_body, sds((FEAT, POS), BF16), 2)(rows, text_embed)


def solution(mesh):
    wide = Mesh(mesh.devices.reshape(2, 2, 2, 8, 4, 2), ("zl", "xh", "xl", "y", "zh", "c"))
    in_specs = (
        P(TP, SEQ),
        P(TP),
        P(TP),
        P(None, TP, SEQ),
        P(TP),
        P(SEQ),
        P(TP, SEQ),
    )
    return jax.shard_map(shards, mesh=wide, in_specs=in_specs, out_specs=P(TP, SEQ), check_vma=False)
```

```python
import functools

import jax
import jax.numpy as jnp
import numpy as np
from jax import lax
from jax.experimental import pallas as pl
from jax.experimental.pallas import tpu as pltpu
from jax.sharding import Mesh
from jax.sharding import PartitionSpec as P

D = 1664
GROUP = 4
N_SEQ = 64
N_TP = 8
FEAT = D // N_TP
TOK = 1024
ROWS = TOK // GROUP
CHUNK = D // N_SEQ
CHUNK_PAD = 32
POS = 384
CAP = 10
SLOTS = 24
HALF = FEAT // 2
LANES = 128
SHARE = ("zl", "xl")
SEQ = ("zl", "xh", "xl", "y")
TP = ("zh", "c")
BF16 = jnp.bfloat16
F32 = jnp.float32


def _vmem(n):
    return [pl.BlockSpec(memory_space=pltpu.VMEM)] * n


def _call(body, outs, n_in, n_smem=0):
    return pl.pallas_call(
        body,
        out_shape=outs,
        in_specs=[pl.BlockSpec(memory_space=pltpu.SMEM)] * n_smem + _vmem(n_in),
        out_specs=jax.tree.map(lambda _: pl.BlockSpec(memory_space=pltpu.VMEM), outs),
        compiler_params=pltpu.CompilerParams(vmem_limit_bytes=48 << 20),
    )


def split_body(x_ref, xd_ref, st_ref):
    row = lax.broadcasted_iota(jnp.int32, (512, 512), 0)
    col = lax.broadcasted_iota(jnp.int32, (512, 512), 1)
    pick = jnp.where(row == 4 * (col & 127) + (col >> 7), 1.0, 0.0).astype(BF16)
    for half in range(2):
        lanes = pl.ds(half * 128, 128)
        moved = jnp.dot(x_ref[:, pl.ds(half * 512, 512)], pick, preferred_element_type=F32)
        for k in range(GROUP):
            block = moved[:, k * 128 : (k + 1) * 128]
            xd_ref[pl.ds(k * FEAT, FEAT), lanes] = block.astype(BF16)
            mean = jnp.sum(block, axis=0, keepdims=True) * (1.0 / FEAT)
            off = block - mean
            st_ref[pl.ds(k, 1), lanes] = mean
            st_ref[pl.ds(GROUP + k, 1), lanes] = jnp.sum(off * off, axis=0, keepdims=True)


def project_body(
    ids, own, rx, rk, rs, st, gain, bias, wg, pack, keep_ref, send_ref, normed, weight
):
    c, q = ids[0], ids[1]
    for g in range(2):
        rows = jnp.concatenate([wg[y, g ^ ids[2]] for y in range(8)], axis=0)
        weight[g] = jnp.dot(pack[...], rows, preferred_element_type=F32).astype(BF16)
    gain_col = jnp.broadcast_to(gain[...], (FEAT, ROWS))
    bias_col = jnp.broadcast_to(bias[...], (FEAT, ROWS))
    for job in range(4):
        kept, i = job // 2 == 1, job % 2
        e = 2 * (c if kept else 1 - c) + i
        parts = st[q ^ e]
        mean = jnp.sum(parts[:, :GROUP], axis=0) * (1.0 / N_TP)
        off = parts[:, :GROUP] - mean[None]
        var = (jnp.sum(parts[:, GROUP:], axis=0) + FEAT * jnp.sum(off * off, axis=0)) * (1.0 / D)
        scale = lax.rsqrt(var + 1e-06)
        for k in range(GROUP):
            at = pl.ds(k * FEAT, FEAT)
            if i == 1:
                x = (rk if kept else rs)[at, :]
            else:
                x = jnp.where((c == 1) == kept, rx[at, :], own[at, :])
            centered = x.astype(F32) - mean[k : k + 1]
            normed[at, :] = (centered * scale[k : k + 1] * gain_col + bias_col).astype(BF16)
        for g in range(2):
            out = jnp.dot(weight[g], normed[...], preferred_element_type=F32).astype(BF16)
            (keep_ref if kept else send_ref)[2 * i + g] = out


def pair_body(ids, keep, got, *outs):
    zh = ids[0]
    for k in range(4):
        p = zh ^ k
        outs[k][...] = (keep[p].astype(F32) + got[p].astype(F32)).astype(BF16)


def place_body(z0, z1, z2, z3, bias, slot, extra, send_ref):
    total = (z0[...].astype(F32) + z1[...].astype(F32)) + (z2[...].astype(F32) + z3[...].astype(F32))
    merged = total + bias[...]
    fill = jnp.zeros((LANES - HALF - 8, ROWS), F32)
    row = lax.broadcasted_iota(jnp.int32, (N_SEQ * SLOTS, ROWS), 0)
    tag_row = lax.broadcasted_iota(jnp.int32, (8, ROWS), 0)
    out = None
    for h in range(2):
        tag = jnp.where(tag_row == 3, float(h), extra[...])
        data = jnp.concatenate([merged[h * HALF : (h + 1) * HALF], tag, fill], axis=0)
        pick = jnp.where(row == slot[...] + h * CAP, 1.0, 0.0).astype(BF16)
        part = lax.dot_general(
            pick, data.astype(BF16), (((1,), (1,)), ((), ())), preferred_element_type=F32
        )
        out = part if out is None else out + part
    send_ref[...] = out.astype(BF16).reshape(N_SEQ, SLOTS, LANES)


def final_body(got, text, out_ref):
    rows = got[...].reshape(N_SEQ * SLOTS, LANES)
    tags = rows.astype(F32)
    at = tags[:, HALF : HALF + 1] * 16.0 + tags[:, HALF + 1 : HALF + 2] - 16.0
    side = tags[:, HALF + 3 : HALF + 4]
    want = lax.broadcasted_iota(jnp.int32, (N_SEQ * SLOTS, POS), 1).astype(F32)
    halves = []
    for h in range(2):
        mine = jnp.where(side == float(h), at, -1.0)
        pick = jnp.where(want == mine, 1.0, 0.0).astype(BF16)
        halves.append(
            lax.dot_general(rows, pick, (((0,), (0,)), ((), ())), preferred_element_type=F32)
        )
    hit = halves[0][HALF + 2 : HALF + 3] > 0.5
    full = jnp.concatenate([halves[0][:HALF], halves[1][:HALF]], axis=0)
    out_ref[...] = jnp.where(hit, full, text[...].astype(F32)).astype(BF16)


def _pairs(sizes, dest):
    return [
        (int(np.ravel_multi_index(at, sizes)), int(np.ravel_multi_index(dest(*at), sizes)))
        for at in np.ndindex(*sizes)
    ]


def shards(patches, ln_gain, ln_bias, merge_weight, merge_bias, targets, text_embed):
    sds = jax.ShapeDtypeStruct
    zl, xh, xl, zh, c = (lax.axis_index(a) for a in ("zl", "xh", "xl", "zh", "c"))

    chunk = jnp.transpose(merge_weight, (2, 0, 1)).reshape(CHUNK, GROUP * FEAT)
    chunk = jnp.pad(chunk, ((0, CHUNK_PAD - CHUNK), (0, 0)))
    other = lax.ppermute(chunk, "xh", [(0, 1), (1, 0)])
    columns = lax.all_gather(jnp.stack([chunk, other]), "y")

    own, stats = _call(split_body, (sds((GROUP * FEAT, ROWS), BF16), sds((8, ROWS), F32)), 1)(patches)
    axes, sizes = ("zl", "xl", "c"), (2, 2, 2)
    rx = lax.ppermute(own, axes, _pairs(sizes, lambda z, x, k: (z ^ 1, x, k)))
    rk = lax.ppermute(own, axes, _pairs(sizes, lambda z, x, k: (z ^ k, x ^ 1, k)))
    rs = lax.ppermute(own, axes, _pairs(sizes, lambda z, x, k: (z ^ k ^ 1, x ^ 1, k)))
    all_stats = lax.all_to_all(
        jnp.broadcast_to(stats[None], (32, 8, ROWS)), SHARE + TP, 0, 0, tiled=True
    ).reshape(4, N_TP, 8, ROWS)

    packed = np.arange(FEAT)
    pack = np.zeros((FEAT, 8 * CHUNK_PAD), np.float32)
    pack[packed, packed // CHUNK * CHUNK_PAD + packed % CHUNK] = 1.0
    ids = jnp.stack([c, 2 * zl + xl, xh]).astype(jnp.int32)
    piece = sds((4, FEAT, ROWS), BF16)
    keep, send = pl.pallas_call(
        project_body,
        out_shape=(piece, piece),
        in_specs=[pl.BlockSpec(memory_space=pltpu.SMEM)] + _vmem(9),
        out_specs=tuple(_vmem(2)),
        scratch_shapes=[
            pltpu.VMEM((GROUP * FEAT, ROWS), BF16),
            pltpu.VMEM((2, FEAT, GROUP * FEAT), BF16),
        ],
        compiler_params=pltpu.CompilerParams(vmem_limit_bytes=48 << 20),
    )(
        ids, own, rx, rk, rs, all_stats,
        ln_gain.astype(F32)[:, None], ln_bias.astype(F32)[:, None], columns, jnp.asarray(pack, BF16),
    )

    got = lax.ppermute(send, "c", [(0, 1), (1, 0)])
    part = sds((FEAT, ROWS), BF16)
    parts = _call(pair_body, (part,) * 4, 2, 1)(zh[None].astype(jnp.int32), keep, got)
    axes, sizes = ("zl", "xl", "zh", "c"), (2, 2, 4, 2)
    moved = [
        lax.ppermute(
            parts[k],
            axes,
            _pairs(sizes, lambda z, x, h, k2, k=k: (z ^ k2, x ^ ((h ^ k) >> 1), 2 * z + ((h ^ k) & 1), x)),
        )
        for k in range(4)
    ]

    target_dev = targets // POS
    local_pos = targets % POS
    before = jnp.arange(ROWS)[:, None] < jnp.arange(ROWS)[None, :]
    rank = jnp.sum(((target_dev[:, None] == target_dev[None, :]) & before).astype(jnp.int32), axis=0)
    slot = (target_dev * SLOTS + rank)[None, :]
    zero = jnp.zeros((ROWS,), F32)
    one = jnp.ones((ROWS,), F32)
    tags = [(local_pos // 16 + 1).astype(F32), (local_pos % 16).astype(F32), one, zero, zero, zero, zero, zero]
    extra = jnp.stack(tags)

    sent = _call(place_body, sds((N_SEQ, SLOTS, LANES), BF16), 7)(
        *moved, merge_bias.astype(F32)[:, None], slot, extra
    )
    rows = lax.all_to_all(sent, SEQ, 0, 0, tiled=True)
    return _call(final_body, sds((FEAT, POS), BF16), 2)(rows, text_embed)


def solution(mesh):
    wide = Mesh(mesh.devices.reshape(2, 2, 2, 8, 4, 2), ("zl", "xh", "xl", "y", "zh", "c"))
    in_specs = (
        P(TP, SEQ),
        P(TP),
        P(TP),
        P(None, TP, SEQ),
        P(TP),
        P(SEQ),
        P(TP, SEQ),
    )
    return jax.shard_map(shards, mesh=wide, in_specs=in_specs, out_specs=P(TP, SEQ), check_vma=False)
```

```python
import functools

import jax
import jax.numpy as jnp
import numpy as np
from jax import lax
from jax.experimental import pallas as pl
from jax.experimental.pallas import tpu as pltpu
from jax.sharding import Mesh
from jax.sharding import PartitionSpec as P

D = 1664
GROUP = 4
N_SEQ = 64
N_TP = 8
FEAT = D // N_TP
TOK = 1024
ROWS = TOK // GROUP
CHUNK = D // N_SEQ
CHUNK_PAD = 32
POS = 384
CAP = 10
SLOTS = 24
HALF = FEAT // 2
LANES = 128
SEQ = ("zl", "xh", "xl", "y")
TP = ("zh", "c")
BF16 = jnp.bfloat16
F32 = jnp.float32


def _vmem(n):
    return [pl.BlockSpec(memory_space=pltpu.VMEM)] * n


def _call(body, outs, n_in, n_smem=0):
    return pl.pallas_call(
        body,
        out_shape=outs,
        in_specs=[pl.BlockSpec(memory_space=pltpu.SMEM)] * n_smem + _vmem(n_in),
        out_specs=jax.tree.map(lambda _: pl.BlockSpec(memory_space=pltpu.VMEM), outs),
        compiler_params=pltpu.CompilerParams(vmem_limit_bytes=48 << 20),
    )


def split_body(x_ref, xd_ref, st_ref):
    row = lax.broadcasted_iota(jnp.int32, (512, 512), 0)
    col = lax.broadcasted_iota(jnp.int32, (512, 512), 1)
    pick = jnp.where(row == 4 * (col & 127) + (col >> 7), 1.0, 0.0).astype(BF16)
    for half in range(2):
        lanes = pl.ds(half * 128, 128)
        moved = jnp.dot(x_ref[:, pl.ds(half * 512, 512)], pick, preferred_element_type=F32)
        for k in range(GROUP):
            block = moved[:, k * 128 : (k + 1) * 128]
            xd_ref[pl.ds(k * FEAT, FEAT), lanes] = block.astype(BF16)
            mean = jnp.sum(block, axis=0, keepdims=True) * (1.0 / FEAT)
            off = block - mean
            st_ref[pl.ds(k, 1), lanes] = mean
            st_ref[pl.ds(GROUP + k, 1), lanes] = jnp.sum(off * off, axis=0, keepdims=True)


def norm_body(x_ref, st, gain, bias, out_ref):
    gain_col = jnp.broadcast_to(gain[...], (FEAT, ROWS))
    bias_col = jnp.broadcast_to(bias[...], (FEAT, ROWS))
    parts = st[...]
    mean = jnp.sum(parts[:, :GROUP], axis=0) * (1.0 / N_TP)
    off = parts[:, :GROUP] - mean[None]
    var = (jnp.sum(parts[:, GROUP:], axis=0) + FEAT * jnp.sum(off * off, axis=0)) * (1.0 / D)
    scale = lax.rsqrt(var + 1e-06)
    for k in range(GROUP):
        at = pl.ds(k * FEAT, FEAT)
        centered = x_ref[at, :].astype(F32) - mean[k : k + 1]
        out_ref[at, :] = (centered * scale[k : k + 1] * gain_col + bias_col).astype(BF16)


def project_body(ids, own, rx, rk, rs, wg, pack, keep_ref, send_ref, weight):
    c, xh = ids[0], ids[1]
    for g in range(2):
        rows = jnp.concatenate([wg[y, g ^ xh] for y in range(8)], axis=0)
        weight[g] = jnp.dot(pack[...], rows, preferred_element_type=F32).astype(BF16)
    for job in range(4):
        kept, i = job // 2 == 1, job % 2
        if i == 1:
            x = (rk if kept else rs)[...]
        else:
            x = jnp.where((c == 1) == kept, rx[...], own[...])
        for g in range(2):
            out = jnp.dot(weight[g], x, preferred_element_type=F32).astype(BF16)
            (keep_ref if kept else send_ref)[2 * i + g] = out


def pair_body(ids, keep, got, *outs):
    zh = ids[0]
    for k in range(4):
        p = zh ^ k
        outs[k][...] = (keep[p].astype(F32) + got[p].astype(F32)).astype(BF16)


def place_body(z0, z1, z2, z3, bias, slot, extra, send_ref):
    total = (z0[...].astype(F32) + z1[...].astype(F32)) + (z2[...].astype(F32) + z3[...].astype(F32))
    merged = total + bias[...]
    fill = jnp.zeros((LANES - HALF - 8, ROWS), F32)
    row = lax.broadcasted_iota(jnp.int32, (N_SEQ * SLOTS, ROWS), 0)
    tag_row = lax.broadcasted_iota(jnp.int32, (8, ROWS), 0)
    out = None
    for h in range(2):
        tag = jnp.where(tag_row == 3, float(h), extra[...])
        data = jnp.concatenate([merged[h * HALF : (h + 1) * HALF], tag, fill], axis=0)
        pick = jnp.where(row == slot[...] + h * CAP, 1.0, 0.0).astype(BF16)
        part = lax.dot_general(
            pick, data.astype(BF16), (((1,), (1,)), ((), ())), preferred_element_type=F32
        )
        out = part if out is None else out + part
    send_ref[...] = out.astype(BF16).reshape(N_SEQ, SLOTS, LANES)


def final_body(got, text, out_ref):
    rows = got[...].reshape(N_SEQ * SLOTS, LANES)
    tags = rows.astype(F32)
    at = tags[:, HALF : HALF + 1] * 16.0 + tags[:, HALF + 1 : HALF + 2] - 16.0
    side = tags[:, HALF + 3 : HALF + 4]
    want = lax.broadcasted_iota(jnp.int32, (N_SEQ * SLOTS, POS), 1).astype(F32)
    halves = []
    for h in range(2):
        mine = jnp.where(side == float(h), at, -1.0)
        pick = jnp.where(want == mine, 1.0, 0.0).astype(BF16)
        halves.append(
            lax.dot_general(rows, pick, (((0,), (0,)), ((), ())), preferred_element_type=F32)
        )
    hit = halves[0][HALF + 2 : HALF + 3] > 0.5
    full = jnp.concatenate([halves[0][:HALF], halves[1][:HALF]], axis=0)
    out_ref[...] = jnp.where(hit, full, text[...].astype(F32)).astype(BF16)


def _pairs(sizes, dest):
    return [
        (int(np.ravel_multi_index(at, sizes)), int(np.ravel_multi_index(dest(*at), sizes)))
        for at in np.ndindex(*sizes)
    ]


def shards(patches, ln_gain, ln_bias, merge_weight, merge_bias, targets, text_embed):
    sds = jax.ShapeDtypeStruct
    xh, zh, c = (lax.axis_index(a) for a in ("xh", "zh", "c"))

    chunk = jnp.transpose(merge_weight, (2, 0, 1)).reshape(CHUNK, GROUP * FEAT)
    chunk = jnp.pad(chunk, ((0, CHUNK_PAD - CHUNK), (0, 0)))
    other = lax.ppermute(chunk, "xh", [(0, 1), (1, 0)])
    columns = lax.all_gather(jnp.stack([chunk, other]), "y")

    own, stats = _call(split_body, (sds((GROUP * FEAT, ROWS), BF16), sds((8, ROWS), F32)), 1)(patches)
    all_stats = lax.all_to_all(jnp.broadcast_to(stats[None], (N_TP, 8, ROWS)), TP, 0, 0, tiled=True)
    own = _call(norm_body, sds((GROUP * FEAT, ROWS), BF16), 4)(
        own, all_stats, ln_gain.astype(F32)[:, None], ln_bias.astype(F32)[:, None]
    )
    axes, sizes = ("zl", "xl", "c"), (2, 2, 2)
    rx = lax.ppermute(own, axes, _pairs(sizes, lambda z, x, k: (z ^ 1, x, k)))
    rk = lax.ppermute(own, axes, _pairs(sizes, lambda z, x, k: (z ^ k, x ^ 1, k)))
    rs = lax.ppermute(own, axes, _pairs(sizes, lambda z, x, k: (z ^ k ^ 1, x ^ 1, k)))

    packed = np.arange(FEAT)
    pack = np.zeros((FEAT, 8 * CHUNK_PAD), np.float32)
    pack[packed, packed // CHUNK * CHUNK_PAD + packed % CHUNK] = 1.0
    ids = jnp.stack([c, xh]).astype(jnp.int32)
    piece = sds((4, FEAT, ROWS), BF16)
    keep, send = pl.pallas_call(
        project_body,
        out_shape=(piece, piece),
        in_specs=[pl.BlockSpec(memory_space=pltpu.SMEM)] + _vmem(6),
        out_specs=tuple(_vmem(2)),
        scratch_shapes=[pltpu.VMEM((2, FEAT, GROUP * FEAT), BF16)],
        compiler_params=pltpu.CompilerParams(vmem_limit_bytes=48 << 20),
    )(ids, own, rx, rk, rs, columns, jnp.asarray(pack, BF16))

    got = lax.ppermute(send, "c", [(0, 1), (1, 0)])
    part = sds((FEAT, ROWS), BF16)
    parts = _call(pair_body, (part,) * 4, 2, 1)(zh[None].astype(jnp.int32), keep, got)
    axes, sizes = ("zl", "xl", "zh", "c"), (2, 2, 4, 2)
    moved = [
        lax.ppermute(
            parts[k],
            axes,
            _pairs(sizes, lambda z, x, h, k2, k=k: (z ^ k2, x ^ ((h ^ k) >> 1), 2 * z + ((h ^ k) & 1), x)),
        )
        for k in range(4)
    ]

    target_dev = targets // POS
    local_pos = targets % POS
    before = jnp.arange(ROWS)[:, None] < jnp.arange(ROWS)[None, :]
    rank = jnp.sum(((target_dev[:, None] == target_dev[None, :]) & before).astype(jnp.int32), axis=0)
    slot = (target_dev * SLOTS + rank)[None, :]
    zero = jnp.zeros((ROWS,), F32)
    one = jnp.ones((ROWS,), F32)
    tags = [(local_pos // 16 + 1).astype(F32), (local_pos % 16).astype(F32), one, zero, zero, zero, zero, zero]
    extra = jnp.stack(tags)

    sent = _call(place_body, sds((N_SEQ, SLOTS, LANES), BF16), 7)(
        *moved, merge_bias.astype(F32)[:, None], slot, extra
    )
    rows = lax.all_to_all(sent, SEQ, 0, 0, tiled=True)
    return _call(final_body, sds((FEAT, POS), BF16), 2)(rows, text_embed)


def solution(mesh):
    wide = Mesh(mesh.devices.reshape(2, 2, 2, 8, 4, 2), ("zl", "xh", "xl", "y", "zh", "c"))
    in_specs = (
        P(TP, SEQ),
        P(TP),
        P(TP),
        P(None, TP, SEQ),
        P(TP),
        P(SEQ),
        P(TP, SEQ),
    )
    return jax.shard_map(shards, mesh=wide, in_specs=in_specs, out_specs=P(TP, SEQ), check_vma=False)
```

```python
import functools

import jax
import jax.numpy as jnp
import numpy as np
from jax import lax
from jax.experimental import pallas as pl
from jax.experimental.pallas import tpu as pltpu
from jax.sharding import Mesh
from jax.sharding import PartitionSpec as P

D = 1664
GROUP = 4
N_SEQ = 64
N_TP = 8
FEAT = D // N_TP
TOK = 1024
ROWS = TOK // GROUP
CHUNK = D // N_SEQ
CHUNK_PAD = 32
POS = 384
CAP = 10
SLOTS = 24
HALF = FEAT // 2
LANES = 128
SEQ = ("zl", "xh", "xl", "yh", "yl")
TP = ("zh", "c")
BF16 = jnp.bfloat16
F32 = jnp.float32


def _vmem(n):
    return [pl.BlockSpec(memory_space=pltpu.VMEM)] * n


def _call(body, outs, n_in, n_smem=0, scratch=()):
    return pl.pallas_call(
        body,
        out_shape=outs,
        in_specs=[pl.BlockSpec(memory_space=pltpu.SMEM)] * n_smem + _vmem(n_in),
        out_specs=jax.tree.map(lambda _: pl.BlockSpec(memory_space=pltpu.VMEM), outs),
        scratch_shapes=scratch,
        compiler_params=pltpu.CompilerParams(vmem_limit_bytes=48 << 20),
    )


def split_body(x_ref, xd_ref, st_ref, part):
    row = lax.broadcasted_iota(jnp.int32, (512, 512), 0)
    col = lax.broadcasted_iota(jnp.int32, (512, 512), 1)
    pick = jnp.where(row == 4 * (col & 127) + (col >> 7), 1.0, 0.0).astype(BF16)
    for half in range(2):
        lanes = pl.ds(half * 128, 128)
        moved = jnp.dot(x_ref[:, pl.ds(half * 512, 512)], pick, preferred_element_type=F32)
        for k in range(GROUP):
            block = moved[:, k * 128 : (k + 1) * 128]
            xd_ref[pl.ds(k * FEAT, FEAT), lanes] = block.astype(BF16)
            mean = jnp.sum(block, axis=0, keepdims=True) * (1.0 / FEAT)
            off = block - mean
            part[pl.ds(k, 1), lanes] = mean
            part[pl.ds(GROUP + k, 1), lanes] = jnp.sum(off * off, axis=0, keepdims=True)
    for t in range(N_TP):
        st_ref[t] = part[...]


def norm_body(x_ref, st, gain, bias, _, out_ref):
    gain_col = jnp.broadcast_to(gain[...], (FEAT, ROWS))
    bias_col = jnp.broadcast_to(bias[...], (FEAT, ROWS))
    parts = st[...]
    mean = jnp.sum(parts[:, :GROUP], axis=0) * (1.0 / N_TP)
    off = parts[:, :GROUP] - mean[None]
    var = (jnp.sum(parts[:, GROUP:], axis=0) + FEAT * jnp.sum(off * off, axis=0)) * (1.0 / D)
    scale = lax.rsqrt(var + 1e-06)
    for k in range(GROUP):
        at = pl.ds(k * FEAT, FEAT)
        centered = x_ref[at, :].astype(F32) - mean[k : k + 1]
        out_ref[at, :] = (centered * scale[k : k + 1] * gain_col + bias_col).astype(BF16)


def pack_body(ids, mine, theirs, pack, out_ref):
    parts = []
    for g in range(2):
        for y in range(2):
            i = g ^ ids[0]
            parts.append(jnp.where(ids[1] == y, mine[i], theirs[i]))
    rows = jnp.concatenate(parts, axis=0)
    out_ref[...] = jnp.dot(pack[...], rows, preferred_element_type=F32).astype(BF16)


def project_body(ids, own, rx, rk, rs, wg, order, keep_ref, send_ref, weight):
    c = ids[0]
    for g in range(2):
        rows = [jnp.dot(order[g, y], wg[y], preferred_element_type=F32) for y in range(4)]
        weight[g] = ((rows[0] + rows[1]) + (rows[2] + rows[3])).astype(BF16)
    for job in range(4):
        kept, i = job // 2 == 1, job % 2
        if i == 1:
            x = (rk if kept else rs)[...]
        else:
            x = jnp.where((c == 1) == kept, rx[...], own[...])
        for g in range(2):
            out = jnp.dot(weight[g], x, preferred_element_type=F32).astype(BF16)
            (keep_ref if kept else send_ref)[2 * i + g] = out


def pair_body(ids, keep, got, *outs):
    zh = ids[0]
    for k in range(4):
        p = zh ^ k
        outs[k][...] = (keep[p].astype(F32) + got[p].astype(F32)).astype(BF16)


def place_body(z0, z1, z2, z3, bias, slot, extra, send_ref):
    total = (z0[...].astype(F32) + z1[...].astype(F32)) + (z2[...].astype(F32) + z3[...].astype(F32))
    merged = total + bias[...]
    fill = jnp.zeros((LANES - HALF - 8, ROWS), F32)
    row = lax.broadcasted_iota(jnp.int32, (N_SEQ * SLOTS, ROWS), 0)
    tag_row = lax.broadcasted_iota(jnp.int32, (8, ROWS), 0)
    out = None
    for h in range(2):
        tag = jnp.where(tag_row == 3, float(h), extra[...])
        data = jnp.concatenate([merged[h * HALF : (h + 1) * HALF], tag, fill], axis=0)
        pick = jnp.where(row == slot[...] + h * CAP, 1.0, 0.0).astype(BF16)
        part = lax.dot_general(
            pick, data.astype(BF16), (((1,), (1,)), ((), ())), preferred_element_type=F32
        )
        out = part if out is None else out + part
    send_ref[...] = out.astype(BF16).reshape(N_SEQ, SLOTS, LANES)


def final_body(got, text, out_ref):
    rows = got[...].reshape(N_SEQ * SLOTS, LANES).astype(F32).T
    at = rows[HALF : HALF + 1] * 16.0 + rows[HALF + 1 : HALF + 2] - 16.0
    side = rows[HALF + 3 : HALF + 4]
    want = lax.broadcasted_iota(jnp.int32, (POS, N_SEQ * SLOTS), 0).astype(F32)
    pick = jnp.where(want == at, 1.0, 0.0).astype(BF16)
    halves = []
    for h in range(2):
        mine = jnp.where(side == float(h), rows, 0.0).astype(BF16)
        halves.append(
            lax.dot_general(mine, pick, (((1,), (1,)), ((), ())), preferred_element_type=F32)
        )
    hit = halves[0][HALF + 2 : HALF + 3] > 0.5
    full = jnp.concatenate([halves[0][:HALF], halves[1][:HALF]], axis=0)
    out_ref[...] = jnp.where(hit, full, text[...].astype(F32)).astype(BF16)


def _pairs(sizes, dest):
    return [
        (int(np.ravel_multi_index(at, sizes)), int(np.ravel_multi_index(dest(*at), sizes)))
        for at in np.ndindex(*sizes)
    ]


def shards(patches, ln_gain, ln_bias, merge_weight, merge_bias, targets, text_embed):
    sds = jax.ShapeDtypeStruct
    xh, yl, zh, c = (lax.axis_index(a) for a in ("xh", "yl", "zh", "c"))

    chunk = jnp.transpose(merge_weight, (2, 0, 1)).reshape(CHUNK, GROUP * FEAT)
    chunk = jnp.pad(chunk, ((0, CHUNK_PAD - CHUNK), (0, 0)))
    pair = jnp.stack([chunk, lax.ppermute(chunk, "xh", [(0, 1), (1, 0)])])
    pair_y = lax.ppermute(pair, "yl", [(0, 1), (1, 0)])
    packed = np.arange(4 * CHUNK)
    pack = np.zeros((4 * CHUNK, 4 * CHUNK_PAD), np.float32)
    pack[packed, packed // CHUNK * CHUNK_PAD + packed % CHUNK] = 1.0
    quad = _call(pack_body, sds((4 * CHUNK, GROUP * FEAT), BF16), 3, 1)(
        jnp.stack([xh, yl]).astype(jnp.int32), pair, pair_y, jnp.asarray(pack, BF16)
    )
    columns = lax.all_gather(quad, "yh")

    own, stats = _call(
        split_body,
        (sds((GROUP * FEAT, ROWS), BF16), sds((N_TP, 8, ROWS), F32)),
        1,
        scratch=[pltpu.VMEM((8, ROWS), F32)],
    )(patches)
    all_stats = lax.all_to_all(stats, TP, 0, 0, tiled=True)
    own = _call(norm_body, sds((GROUP * FEAT, ROWS), BF16), 5)(
        own, all_stats, ln_gain.astype(F32)[:, None], ln_bias.astype(F32)[:, None], pair_y
    )
    axes, sizes = ("zl", "xl", "c"), (2, 2, 2)
    rx = lax.ppermute(own, axes, _pairs(sizes, lambda z, x, k: (z ^ 1, x, k)))
    rk = lax.ppermute(own, axes, _pairs(sizes, lambda z, x, k: (z ^ k, x ^ 1, k)))
    rs = lax.ppermute(own, axes, _pairs(sizes, lambda z, x, k: (z ^ k ^ 1, x ^ 1, k)))

    order = np.zeros((2, 4, FEAT, 4 * CHUNK), np.float32)
    for g in range(2):
        for r in range(FEAT):
            order[g, r // (2 * CHUNK), r, g * 2 * CHUNK + r % (2 * CHUNK)] = 1.0
    ids = c[None].astype(jnp.int32)
    piece = sds((4, FEAT, ROWS), BF16)
    keep, send = pl.pallas_call(
        project_body,
        out_shape=(piece, piece),
        in_specs=[pl.BlockSpec(memory_space=pltpu.SMEM)] + _vmem(6),
        out_specs=tuple(_vmem(2)),
        scratch_shapes=[pltpu.VMEM((2, FEAT, GROUP * FEAT), BF16)],
        compiler_params=pltpu.CompilerParams(vmem_limit_bytes=48 << 20),
    )(ids, own, rx, rk, rs, columns, jnp.asarray(order, BF16))

    got = lax.ppermute(send, "c", [(0, 1), (1, 0)])
    part = sds((FEAT, ROWS), BF16)
    parts = _call(pair_body, (part,) * 4, 2, 1)(zh[None].astype(jnp.int32), keep, got)
    axes, sizes = ("zl", "xl", "zh", "c"), (2, 2, 4, 2)
    moved = [
        lax.ppermute(
            parts[k],
            axes,
            _pairs(sizes, lambda z, x, h, k2, k=k: (z ^ k2, x ^ ((h ^ k) >> 1), 2 * z + ((h ^ k) & 1), x)),
        )
        for k in range(4)
    ]

    target_dev = targets // POS
    local_pos = targets % POS
    before = jnp.arange(ROWS)[:, None] < jnp.arange(ROWS)[None, :]
    rank = jnp.sum(((target_dev[:, None] == target_dev[None, :]) & before).astype(jnp.int32), axis=0)
    slot = (target_dev * SLOTS + rank)[None, :]
    zero = jnp.zeros((ROWS,), F32)
    one = jnp.ones((ROWS,), F32)
    tags = [(local_pos // 16 + 1).astype(F32), (local_pos % 16).astype(F32), one, zero, zero, zero, zero, zero]
    extra = jnp.stack(tags)

    sent = _call(place_body, sds((N_SEQ, SLOTS, LANES), BF16), 7)(
        *moved, merge_bias.astype(F32)[:, None], slot, extra
    )
    rows = lax.all_to_all(sent, SEQ, 0, 0, tiled=True)
    return _call(final_body, sds((FEAT, POS), BF16), 2)(rows, text_embed)


def solution(mesh):
    wide = Mesh(mesh.devices.reshape(2, 2, 2, 4, 2, 4, 2), ("zl", "xh", "xl", "yh", "yl", "zh", "c"))
    in_specs = (
        P(TP, SEQ),
        P(TP),
        P(TP),
        P(None, TP, SEQ),
        P(TP),
        P(SEQ),
        P(TP, SEQ),
    )
    return jax.shard_map(shards, mesh=wide, in_specs=in_specs, out_specs=P(TP, SEQ), check_vma=False)
```

```python
import functools

import jax
import jax.numpy as jnp
import numpy as np
from jax import lax
from jax.experimental import pallas as pl
from jax.experimental.pallas import tpu as pltpu
from jax.sharding import Mesh
from jax.sharding import PartitionSpec as P

D = 1664
GROUP = 4
N_SEQ = 64
N_TP = 8
FEAT = D // N_TP
TOK = 1024
ROWS = TOK // GROUP
CHUNK = D // N_SEQ
CHUNK_PAD = 32
POS = 384
CAP = 10
SLOTS = 24
HALF = FEAT // 2
LANES = 128
SEQ = ("zl", "xh", "xl", "yh", "yl")
TP = ("zh", "c")
SHARE = ("zl", "xl")
BF16 = jnp.bfloat16
F32 = jnp.float32


def _vmem(n):
    return [pl.BlockSpec(memory_space=pltpu.VMEM)] * n


def _call(body, outs, n_in, n_smem=0, scratch=()):
    return pl.pallas_call(
        body,
        out_shape=outs,
        in_specs=[pl.BlockSpec(memory_space=pltpu.SMEM)] * n_smem + _vmem(n_in),
        out_specs=jax.tree.map(lambda _: pl.BlockSpec(memory_space=pltpu.VMEM), outs),
        scratch_shapes=scratch,
        compiler_params=pltpu.CompilerParams(vmem_limit_bytes=48 << 20),
    )


def split_body(x_ref, xd_ref, st_ref, part):
    row = lax.broadcasted_iota(jnp.int32, (512, 512), 0)
    col = lax.broadcasted_iota(jnp.int32, (512, 512), 1)
    pick = jnp.where(row == 4 * (col & 127) + (col >> 7), 1.0, 0.0).astype(BF16)
    for half in range(2):
        lanes = pl.ds(half * 128, 128)
        moved = jnp.dot(x_ref[:, pl.ds(half * 512, 512)], pick, preferred_element_type=F32)
        for k in range(GROUP):
            block = moved[:, k * 128 : (k + 1) * 128]
            xd_ref[pl.ds(k * FEAT, FEAT), lanes] = block.astype(BF16)
            mean = jnp.sum(block, axis=0, keepdims=True) * (1.0 / FEAT)
            off = block - mean
            part[pl.ds(k, 1), lanes] = mean
            part[pl.ds(GROUP + k, 1), lanes] = jnp.sum(off * off, axis=0, keepdims=True)
    for t in range(N_TP):
        st_ref[t] = part[...]


def norm_body(x_ref, st, gain, bias, _, out_ref):
    gain_col = jnp.broadcast_to(gain[...], (FEAT, ROWS))
    bias_col = jnp.broadcast_to(bias[...], (FEAT, ROWS))
    parts = st[...]
    mean = jnp.sum(parts[:, :GROUP], axis=0) * (1.0 / N_TP)
    off = parts[:, :GROUP] - mean[None]
    var = (jnp.sum(parts[:, GROUP:], axis=0) + FEAT * jnp.sum(off * off, axis=0)) * (1.0 / D)
    scale = lax.rsqrt(var + 1e-06)
    for k in range(GROUP):
        at = pl.ds(k * FEAT, FEAT)
        centered = x_ref[at, :].astype(F32) - mean[k : k + 1]
        block = (centered * scale[k : k + 1] * gain_col + bias_col).astype(BF16)
        for t in range(4):
            out_ref[t, at, :] = block


def pack_body(ids, mine, theirs, pack, out_ref):
    parts = []
    for g in range(2):
        for y in range(2):
            i = g ^ ids[0]
            parts.append(jnp.where(ids[1] == y, mine[i], theirs[i]))
    rows = jnp.concatenate(parts, axis=0)
    out_ref[...] = jnp.dot(pack[...], rows, preferred_element_type=F32).astype(BF16)


def project_body(ids, x_ref, wg, order, keep_ref, send_ref, weight):
    c, q = ids[0], ids[1]
    for g in range(2):
        rows = [jnp.dot(order[g, y], wg[y], preferred_element_type=F32) for y in range(4)]
        weight[g] = ((rows[0] + rows[1]) + (rows[2] + rows[3])).astype(BF16)
    for job in range(4):
        kept, i = job // 2 == 1, job % 2
        x = x_ref[q ^ (2 * (c if kept else 1 - c) + i)]
        for g in range(2):
            out = jnp.dot(weight[g], x, preferred_element_type=F32).astype(BF16)
            (keep_ref if kept else send_ref)[2 * i + g] = out


def pair_body(ids, keep, got, *outs):
    zh = ids[0]
    for k in range(4):
        p = zh ^ k
        outs[k][...] = (keep[p].astype(F32) + got[p].astype(F32)).astype(BF16)


def place_body(z0, z1, z2, z3, bias, slot, extra, send_ref):
    total = (z0[...].astype(F32) + z1[...].astype(F32)) + (z2[...].astype(F32) + z3[...].astype(F32))
    merged = total + bias[...]
    fill = jnp.zeros((LANES - HALF - 8, ROWS), F32)
    row = lax.broadcasted_iota(jnp.int32, (N_SEQ * SLOTS, ROWS), 0)
    tag_row = lax.broadcasted_iota(jnp.int32, (8, ROWS), 0)
    out = None
    for h in range(2):
        tag = jnp.where(tag_row == 3, float(h), extra[...])
        data = jnp.concatenate([merged[h * HALF : (h + 1) * HALF], tag, fill], axis=0)
        pick = jnp.where(row == slot[...] + h * CAP, 1.0, 0.0).astype(BF16)
        part = lax.dot_general(
            pick, data.astype(BF16), (((1,), (1,)), ((), ())), preferred_element_type=F32
        )
        out = part if out is None else out + part
    send_ref[...] = out.astype(BF16).reshape(N_SEQ, SLOTS, LANES)


def final_body(got, text, out_ref):
    rows = got[...].reshape(N_SEQ * SLOTS, LANES).astype(F32).T
    at = rows[HALF : HALF + 1] * 16.0 + rows[HALF + 1 : HALF + 2] - 16.0
    side = rows[HALF + 3 : HALF + 4]
    want = lax.broadcasted_iota(jnp.int32, (POS, N_SEQ * SLOTS), 0).astype(F32)
    pick = jnp.where(want == at, 1.0, 0.0).astype(BF16)
    mine = [jnp.where(side == float(h), rows, 0.0).astype(BF16) for h in range(2)]
    both = lax.dot_general(
        jnp.concatenate(mine, axis=0), pick, (((1,), (1,)), ((), ())), preferred_element_type=F32
    )
    hit = both[HALF + 2 : HALF + 3] > 0.5
    full = jnp.concatenate([both[:HALF], both[LANES : LANES + HALF]], axis=0)
    out_ref[...] = jnp.where(hit, full, text[...].astype(F32)).astype(BF16)


def _pairs(sizes, dest):
    return [
        (int(np.ravel_multi_index(at, sizes)), int(np.ravel_multi_index(dest(*at), sizes)))
        for at in np.ndindex(*sizes)
    ]


def shards(patches, ln_gain, ln_bias, merge_weight, merge_bias, targets, text_embed):
    sds = jax.ShapeDtypeStruct
    zl, xh, xl, yl, zh, c = (lax.axis_index(a) for a in ("zl", "xh", "xl", "yl", "zh", "c"))

    chunk = jnp.transpose(merge_weight, (2, 0, 1)).reshape(CHUNK, GROUP * FEAT)
    chunk = jnp.pad(chunk, ((0, CHUNK_PAD - CHUNK), (0, 0)))
    pair = jnp.stack([chunk, lax.ppermute(chunk, "xh", [(0, 1), (1, 0)])])
    pair_y = lax.ppermute(pair, "yl", [(0, 1), (1, 0)])
    packed = np.arange(4 * CHUNK)
    pack = np.zeros((4 * CHUNK, 4 * CHUNK_PAD), np.float32)
    pack[packed, packed // CHUNK * CHUNK_PAD + packed % CHUNK] = 1.0
    quad = _call(pack_body, sds((4 * CHUNK, GROUP * FEAT), BF16), 3, 1)(
        jnp.stack([xh, yl]).astype(jnp.int32), pair, pair_y, jnp.asarray(pack, BF16)
    )
    columns = lax.all_gather(quad, "yh")

    own, stats = _call(
        split_body,
        (sds((GROUP * FEAT, ROWS), BF16), sds((N_TP, 8, ROWS), F32)),
        1,
        scratch=[pltpu.VMEM((8, ROWS), F32)],
    )(patches)
    all_stats = lax.all_to_all(stats, TP, 0, 0, tiled=True)
    copies = _call(norm_body, sds((4, GROUP * FEAT, ROWS), BF16), 5)(
        own, all_stats, ln_gain.astype(F32)[:, None], ln_bias.astype(F32)[:, None], pair_y
    )
    shared = lax.all_to_all(copies, SHARE, 0, 0, tiled=True)

    order = np.zeros((2, 4, FEAT, 4 * CHUNK), np.float32)
    for g in range(2):
        for r in range(FEAT):
            order[g, r // (2 * CHUNK), r, g * 2 * CHUNK + r % (2 * CHUNK)] = 1.0
    ids = jnp.stack([c, 2 * zl + xl]).astype(jnp.int32)
    piece = sds((4, FEAT, ROWS), BF16)
    keep, send = pl.pallas_call(
        project_body,
        out_shape=(piece, piece),
        in_specs=[pl.BlockSpec(memory_space=pltpu.SMEM)] + _vmem(3),
        out_specs=tuple(_vmem(2)),
        scratch_shapes=[pltpu.VMEM((2, FEAT, GROUP * FEAT), BF16)],
        compiler_params=pltpu.CompilerParams(vmem_limit_bytes=48 << 20),
    )(ids, shared, columns, jnp.asarray(order, BF16))

    got = lax.ppermute(send, "c", [(0, 1), (1, 0)])
    part = sds((FEAT, ROWS), BF16)
    parts = _call(pair_body, (part,) * 4, 2, 1)(zh[None].astype(jnp.int32), keep, got)
    axes, sizes = ("zl", "xl", "zh", "c"), (2, 2, 4, 2)
    moved = [
        lax.ppermute(
            parts[k],
            axes,
            _pairs(sizes, lambda z, x, h, k2, k=k: (z ^ k2, x ^ ((h ^ k) >> 1), 2 * z + ((h ^ k) & 1), x)),
        )
        for k in (2, 3, 1, 0)
    ]

    target_dev = targets // POS
    local_pos = targets % POS
    before = jnp.arange(ROWS)[:, None] < jnp.arange(ROWS)[None, :]
    rank = jnp.sum(((target_dev[:, None] == target_dev[None, :]) & before).astype(jnp.int32), axis=0)
    slot = (target_dev * SLOTS + rank)[None, :]
    zero = jnp.zeros((ROWS,), F32)
    one = jnp.ones((ROWS,), F32)
    tags = [(local_pos // 16 + 1).astype(F32), (local_pos % 16).astype(F32), one, zero, zero, zero, zero, zero]
    extra = jnp.stack(tags)

    sent = _call(place_body, sds((N_SEQ, SLOTS, LANES), BF16), 7)(
        *moved, merge_bias.astype(F32)[:, None], slot, extra
    )
    rows = lax.all_to_all(sent, SEQ, 0, 0, tiled=True)
    return _call(final_body, sds((FEAT, POS), BF16), 2)(rows, text_embed)


def solution(mesh):
    wide = Mesh(mesh.devices.reshape(2, 2, 2, 4, 2, 4, 2), ("zl", "xh", "xl", "yh", "yl", "zh", "c"))
    in_specs = (
        P(TP, SEQ),
        P(TP),
        P(TP),
        P(None, TP, SEQ),
        P(TP),
        P(SEQ),
        P(TP, SEQ),
    )
    return jax.shard_map(shards, mesh=wide, in_specs=in_specs, out_specs=P(TP, SEQ), check_vma=False)
```

```python
import functools

import jax
import jax.numpy as jnp
import numpy as np
from jax import lax
from jax.experimental import pallas as pl
from jax.experimental.pallas import tpu as pltpu
from jax.sharding import Mesh
from jax.sharding import PartitionSpec as P

D = 1664
GROUP = 4
N_SEQ = 64
N_TP = 8
FEAT = D // N_TP
TOK = 1024
ROWS = TOK // GROUP
CHUNK = D // N_SEQ
CHUNK_PAD = 32
POS = 384
CAP = 10
SLOTS = 24
HALF = FEAT // 2
LANES = 128
SEQ = ("zl", "xh", "xl", "yh", "yl")
TP = ("zh", "c")
SHARE = ("zl", "xl")
BF16 = jnp.bfloat16
F32 = jnp.float32


def _vmem(n):
    return [pl.BlockSpec(memory_space=pltpu.VMEM)] * n


def _call(body, outs, n_in, n_smem=0, scratch=()):
    return pl.pallas_call(
        body,
        out_shape=outs,
        in_specs=[pl.BlockSpec(memory_space=pltpu.SMEM)] * n_smem + _vmem(n_in),
        out_specs=jax.tree.map(lambda _: pl.BlockSpec(memory_space=pltpu.VMEM), outs),
        scratch_shapes=scratch,
        compiler_params=pltpu.CompilerParams(vmem_limit_bytes=48 << 20),
    )


def split_body(x_ref, xd_ref, st_ref, part):
    row = lax.broadcasted_iota(jnp.int32, (512, 512), 0)
    col = lax.broadcasted_iota(jnp.int32, (512, 512), 1)
    pick = jnp.where(row == 4 * (col & 127) + (col >> 7), 1.0, 0.0).astype(BF16)
    for half in range(2):
        lanes = pl.ds(half * 128, 128)
        moved = jnp.dot(x_ref[:, pl.ds(half * 512, 512)], pick, preferred_element_type=F32)
        for k in range(GROUP):
            block = moved[:, k * 128 : (k + 1) * 128]
            xd_ref[pl.ds(k * FEAT, FEAT), lanes] = block.astype(BF16)
            mean = jnp.sum(block, axis=0, keepdims=True) * (1.0 / FEAT)
            off = block - mean
            part[pl.ds(k, 1), lanes] = mean
            part[pl.ds(GROUP + k, 1), lanes] = jnp.sum(off * off, axis=0, keepdims=True)
    for t in range(N_TP):
        st_ref[t] = part[...]


def norm_body(x_ref, st, gain, bias, _, out_ref, held, sem):
    gain_col = jnp.broadcast_to(gain[...], (FEAT, ROWS))
    bias_col = jnp.broadcast_to(bias[...], (FEAT, ROWS))
    parts = st[...]
    mean = jnp.sum(parts[:, :GROUP], axis=0) * (1.0 / N_TP)
    off = parts[:, :GROUP] - mean[None]
    var = (jnp.sum(parts[:, GROUP:], axis=0) + FEAT * jnp.sum(off * off, axis=0)) * (1.0 / D)
    scale = lax.rsqrt(var + 1e-06)
    copies = []
    for k in range(GROUP):
        at = pl.ds(k * FEAT, FEAT)
        centered = x_ref[at, :].astype(F32) - mean[k : k + 1]
        held[at, :] = (centered * scale[k : k + 1] * gain_col + bias_col).astype(BF16)
        for t in range(4):
            copy = pltpu.make_async_copy(held.at[at, :], out_ref.at[t, at, :], sem.at[k, t])
            copy.start()
            copies.append(copy)
    for copy in copies:
        copy.wait()


def pack_body(ids, mine, theirs, pack, out_ref):
    parts = []
    for g in range(2):
        for y in range(2):
            i = g ^ ids[0]
            parts.append(jnp.where(ids[1] == y, mine[i], theirs[i]))
    rows = jnp.concatenate(parts, axis=0)
    out_ref[...] = jnp.dot(pack[...], rows, preferred_element_type=F32).astype(BF16)


def project_body(ids, x_ref, wg, order, keep_ref, send_ref, weight):
    c, q = ids[0], ids[1]
    for g in range(2):
        rows = [jnp.dot(order[g, y], wg[y], preferred_element_type=F32) for y in range(4)]
        weight[g] = ((rows[0] + rows[1]) + (rows[2] + rows[3])).astype(BF16)
    for job in range(4):
        kept, i = job // 2 == 1, job % 2
        x = x_ref[q ^ (2 * (c if kept else 1 - c) + i)]
        for g in range(2):
            out = jnp.dot(weight[g], x, preferred_element_type=F32).astype(BF16)
            (keep_ref if kept else send_ref)[2 * i + g] = out


def pair_body(ids, keep, got, *outs):
    zh = ids[0]
    for k in range(4):
        p = zh ^ k
        outs[k][...] = (keep[p].astype(F32) + got[p].astype(F32)).astype(BF16)


def place_body(z0, z1, z2, z3, bias, slot, extra, send_ref):
    total = (z0[...].astype(F32) + z1[...].astype(F32)) + (z2[...].astype(F32) + z3[...].astype(F32))
    merged = total + bias[...]
    fill = jnp.zeros((LANES - HALF - 8, ROWS), F32)
    row = lax.broadcasted_iota(jnp.int32, (N_SEQ * SLOTS, ROWS), 0)
    tag_row = lax.broadcasted_iota(jnp.int32, (8, ROWS), 0)
    out = None
    for h in range(2):
        tag = jnp.where(tag_row == 3, float(h), extra[...])
        data = jnp.concatenate([merged[h * HALF : (h + 1) * HALF], tag, fill], axis=0)
        pick = jnp.where(row == slot[...] + h * CAP, 1.0, 0.0).astype(BF16)
        part = lax.dot_general(
            pick, data.astype(BF16), (((1,), (1,)), ((), ())), preferred_element_type=F32
        )
        out = part if out is None else out + part
    send_ref[...] = out.astype(BF16).reshape(N_SEQ, SLOTS, LANES)


def final_body(got, text, out_ref):
    rows = got[...].reshape(N_SEQ * SLOTS, LANES).astype(F32).T
    at = rows[HALF : HALF + 1] * 16.0 + rows[HALF + 1 : HALF + 2] - 16.0
    side = rows[HALF + 3 : HALF + 4]
    want = lax.broadcasted_iota(jnp.int32, (POS, N_SEQ * SLOTS), 0).astype(F32)
    pick = jnp.where(want == at, 1.0, 0.0).astype(BF16)
    mine = [jnp.where(side == float(h), rows, 0.0).astype(BF16) for h in range(2)]
    both = lax.dot_general(
        jnp.concatenate(mine, axis=0), pick, (((1,), (1,)), ((), ())), preferred_element_type=F32
    )
    hit = both[HALF + 2 : HALF + 3] > 0.5
    full = jnp.concatenate([both[:HALF], both[LANES : LANES + HALF]], axis=0)
    out_ref[...] = jnp.where(hit, full, text[...].astype(F32)).astype(BF16)


def _pairs(sizes, dest):
    return [
        (int(np.ravel_multi_index(at, sizes)), int(np.ravel_multi_index(dest(*at), sizes)))
        for at in np.ndindex(*sizes)
    ]


def shards(patches, ln_gain, ln_bias, merge_weight, merge_bias, targets, text_embed):
    sds = jax.ShapeDtypeStruct
    zl, xh, xl, yl, zh, c = (lax.axis_index(a) for a in ("zl", "xh", "xl", "yl", "zh", "c"))

    chunk = jnp.transpose(merge_weight, (2, 0, 1)).reshape(CHUNK, GROUP * FEAT)
    chunk = jnp.pad(chunk, ((0, CHUNK_PAD - CHUNK), (0, 0)))
    pair = jnp.stack([chunk, lax.ppermute(chunk, "xh", [(0, 1), (1, 0)])])
    pair_y = lax.ppermute(pair, "yl", [(0, 1), (1, 0)])
    packed = np.arange(4 * CHUNK)
    pack = np.zeros((4 * CHUNK, 4 * CHUNK_PAD), np.float32)
    pack[packed, packed // CHUNK * CHUNK_PAD + packed % CHUNK] = 1.0
    quad = _call(pack_body, sds((4 * CHUNK, GROUP * FEAT), BF16), 3, 1)(
        jnp.stack([xh, yl]).astype(jnp.int32), pair, pair_y, jnp.asarray(pack, BF16)
    )
    columns = lax.all_gather(quad, "yh")

    own, stats = _call(
        split_body,
        (sds((GROUP * FEAT, ROWS), BF16), sds((N_TP, 8, ROWS), F32)),
        1,
        scratch=[pltpu.VMEM((8, ROWS), F32)],
    )(patches)
    all_stats = lax.all_to_all(stats, TP, 0, 0, tiled=True)
    copies = pl.pallas_call(
        norm_body,
        out_shape=sds((4, GROUP * FEAT, ROWS), BF16),
        in_specs=_vmem(5),
        out_specs=pl.BlockSpec(memory_space=pltpu.HBM),
        scratch_shapes=[
            pltpu.VMEM((GROUP * FEAT, ROWS), BF16),
            pltpu.SemaphoreType.DMA((GROUP, 4)),
        ],
        compiler_params=pltpu.CompilerParams(vmem_limit_bytes=48 << 20),
    )(own, all_stats, ln_gain.astype(F32)[:, None], ln_bias.astype(F32)[:, None], pair_y)
    shared = lax.all_to_all(copies, SHARE, 0, 0, tiled=True)

    order = np.zeros((2, 4, FEAT, 4 * CHUNK), np.float32)
    for g in range(2):
        for r in range(FEAT):
            order[g, r // (2 * CHUNK), r, g * 2 * CHUNK + r % (2 * CHUNK)] = 1.0
    ids = jnp.stack([c, 2 * zl + xl]).astype(jnp.int32)
    piece = sds((4, FEAT, ROWS), BF16)
    keep, send = pl.pallas_call(
        project_body,
        out_shape=(piece, piece),
        in_specs=[pl.BlockSpec(memory_space=pltpu.SMEM)] + _vmem(3),
        out_specs=tuple(_vmem(2)),
        scratch_shapes=[pltpu.VMEM((2, FEAT, GROUP * FEAT), BF16)],
        compiler_params=pltpu.CompilerParams(vmem_limit_bytes=48 << 20),
    )(ids, shared, columns, jnp.asarray(order, BF16))

    got = lax.ppermute(send, "c", [(0, 1), (1, 0)])
    part = sds((FEAT, ROWS), BF16)
    parts = _call(pair_body, (part,) * 4, 2, 1)(zh[None].astype(jnp.int32), keep, got)
    axes, sizes = ("zl", "xl", "zh", "c"), (2, 2, 4, 2)
    moved = [
        lax.ppermute(
            parts[k],
            axes,
            _pairs(sizes, lambda z, x, h, k2, k=k: (z ^ k2, x ^ ((h ^ k) >> 1), 2 * z + ((h ^ k) & 1), x)),
        )
        for k in (2, 3, 1, 0)
    ]

    target_dev = targets // POS
    local_pos = targets % POS
    before = jnp.arange(ROWS)[:, None] < jnp.arange(ROWS)[None, :]
    rank = jnp.sum(((target_dev[:, None] == target_dev[None, :]) & before).astype(jnp.int32), axis=0)
    slot = (target_dev * SLOTS + rank)[None, :]
    zero = jnp.zeros((ROWS,), F32)
    one = jnp.ones((ROWS,), F32)
    tags = [(local_pos // 16 + 1).astype(F32), (local_pos % 16).astype(F32), one, zero, zero, zero, zero, zero]
    extra = jnp.stack(tags)

    sent = _call(place_body, sds((N_SEQ, SLOTS, LANES), BF16), 7)(
        *moved, merge_bias.astype(F32)[:, None], slot, extra
    )
    rows = lax.all_to_all(sent, SEQ, 0, 0, tiled=True)
    return _call(final_body, sds((FEAT, POS), BF16), 2)(rows, text_embed)


def solution(mesh):
    wide = Mesh(mesh.devices.reshape(2, 2, 2, 4, 2, 4, 2), ("zl", "xh", "xl", "yh", "yl", "zh", "c"))
    in_specs = (
        P(TP, SEQ),
        P(TP),
        P(TP),
        P(None, TP, SEQ),
        P(TP),
        P(SEQ),
        P(TP, SEQ),
    )
    return jax.shard_map(shards, mesh=wide, in_specs=in_specs, out_specs=P(TP, SEQ), check_vma=False)
```

```python
import functools

import jax
import jax.numpy as jnp
import numpy as np
from jax import lax
from jax.experimental import pallas as pl
from jax.experimental.pallas import tpu as pltpu
from jax.sharding import Mesh
from jax.sharding import PartitionSpec as P

D = 1664
GROUP = 4
N_SEQ = 64
N_TP = 8
FEAT = D // N_TP
TOK = 1024
ROWS = TOK // GROUP
CHUNK = D // N_SEQ
CHUNK_PAD = 32
POS = 384
CAP = 10
SLOTS = 24
HALF = FEAT // 2
LANES = 128
SEQ = ("zl", "xh", "xl", "yh", "yl")
TP = ("zh", "c")
SHARE = ("zl", "xl")
BF16 = jnp.bfloat16
F32 = jnp.float32


def _vmem(n):
    return [pl.BlockSpec(memory_space=pltpu.VMEM)] * n


def _call(body, outs, n_in, n_smem=0, scratch=()):
    return pl.pallas_call(
        body,
        out_shape=outs,
        in_specs=[pl.BlockSpec(memory_space=pltpu.SMEM)] * n_smem + _vmem(n_in),
        out_specs=jax.tree.map(lambda _: pl.BlockSpec(memory_space=pltpu.VMEM), outs),
        scratch_shapes=scratch,
        compiler_params=pltpu.CompilerParams(vmem_limit_bytes=48 << 20),
    )


def split_body(x_ref, xd_ref, st_ref, part):
    row = lax.broadcasted_iota(jnp.int32, (512, 512), 0)
    col = lax.broadcasted_iota(jnp.int32, (512, 512), 1)
    pick = jnp.where(row == 4 * (col & 127) + (col >> 7), 1.0, 0.0).astype(BF16)
    for half in range(2):
        lanes = pl.ds(half * 128, 128)
        moved = jnp.dot(x_ref[:, pl.ds(half * 512, 512)], pick, preferred_element_type=F32)
        for k in range(GROUP):
            block = moved[:, k * 128 : (k + 1) * 128]
            xd_ref[pl.ds(k * FEAT, FEAT), lanes] = block.astype(BF16)
            mean = jnp.sum(block, axis=0, keepdims=True) * (1.0 / FEAT)
            off = block - mean
            part[pl.ds(k, 1), lanes] = mean
            part[pl.ds(GROUP + k, 1), lanes] = jnp.sum(off * off, axis=0, keepdims=True)
    for t in range(N_TP):
        st_ref[t] = part[...]


def norm_body(x_ref, st, gain, bias, _, out_ref, held, sem):
    gain_col = jnp.broadcast_to(gain[...], (FEAT, ROWS))
    bias_col = jnp.broadcast_to(bias[...], (FEAT, ROWS))
    parts = st[...]
    mean = jnp.sum(parts[:, :GROUP], axis=0) * (1.0 / N_TP)
    off = parts[:, :GROUP] - mean[None]
    var = (jnp.sum(parts[:, GROUP:], axis=0) + FEAT * jnp.sum(off * off, axis=0)) * (1.0 / D)
    scale = lax.rsqrt(var + 1e-06)
    copies = []
    for k in range(GROUP):
        at = pl.ds(k * FEAT, FEAT)
        centered = x_ref[at, :].astype(F32) - mean[k : k + 1]
        held[at, :] = (centered * scale[k : k + 1] * gain_col + bias_col).astype(BF16)
        for t in range(4):
            copy = pltpu.make_async_copy(held.at[at, :], out_ref.at[t, at, :], sem.at[k, t])
            copy.start()
            copies.append(copy)
    for copy in copies:
        copy.wait()


def pack_body(ids, mine, theirs, pack, out_ref):
    parts = []
    for g in range(2):
        for y in range(2):
            i = g ^ ids[0]
            parts.append(jnp.where(ids[1] == y, mine[i], theirs[i]))
    rows = jnp.concatenate(parts, axis=0)
    out_ref[...] = jnp.dot(pack[...], rows, preferred_element_type=F32).astype(BF16)


def project_body(ids, x_ref, wg, order, send_ref, keep_ref, weight):
    c, q = ids[0], ids[1]
    for g in range(2):
        rows = [jnp.dot(order[g, y], wg[y], preferred_element_type=F32) for y in range(4)]
        weight[g] = ((rows[0] + rows[1]) + (rows[2] + rows[3])).astype(BF16)
    for job in range(4):
        kept, i = job // 2 == 1, job % 2
        x = x_ref[q ^ (2 * (c if kept else 1 - c) + i)]
        for g in range(2):
            out = jnp.dot(weight[g], x, preferred_element_type=F32).astype(BF16)
            (keep_ref if kept else send_ref)[2 * i + g] = out


def pair_body(ids, keep, got, *outs):
    zh = ids[0]
    for k in range(4):
        p = zh ^ k
        outs[k][...] = (keep[p].astype(F32) + got[p].astype(F32)).astype(BF16)


def place_body(z0, z1, z2, z3, bias, slot, extra, send_ref):
    total = (z0[...].astype(F32) + z1[...].astype(F32)) + (z2[...].astype(F32) + z3[...].astype(F32))
    merged = total + bias[...]
    fill = jnp.zeros((LANES - HALF - 8, ROWS), F32)
    row = lax.broadcasted_iota(jnp.int32, (N_SEQ * SLOTS, ROWS), 0)
    tag_row = lax.broadcasted_iota(jnp.int32, (8, ROWS), 0)
    out = None
    for h in range(2):
        tag = jnp.where(tag_row == 3, float(h), extra[...])
        data = jnp.concatenate([merged[h * HALF : (h + 1) * HALF], tag, fill], axis=0)
        pick = jnp.where(row == slot[...] + h * CAP, 1.0, 0.0).astype(BF16)
        part = lax.dot_general(
            pick, data.astype(BF16), (((1,), (1,)), ((), ())), preferred_element_type=F32
        )
        out = part if out is None else out + part
    send_ref[...] = out.astype(BF16).reshape(N_SEQ, SLOTS, LANES)


def final_body(got, text, out_ref):
    rows = got[...].reshape(N_SEQ * SLOTS, LANES).astype(F32).T
    at = rows[HALF : HALF + 1] * 16.0 + rows[HALF + 1 : HALF + 2] - 16.0
    side = rows[HALF + 3 : HALF + 4]
    want = lax.broadcasted_iota(jnp.int32, (POS, N_SEQ * SLOTS), 0).astype(F32)
    pick = jnp.where(want == at, 1.0, 0.0).astype(BF16)
    mine = [jnp.where(side == float(h), rows, 0.0).astype(BF16) for h in range(2)]
    both = lax.dot_general(
        jnp.concatenate(mine, axis=0), pick, (((1,), (1,)), ((), ())), preferred_element_type=F32
    )
    hit = both[HALF + 2 : HALF + 3] > 0.5
    full = jnp.concatenate([both[:HALF], both[LANES : LANES + HALF]], axis=0)
    out_ref[...] = jnp.where(hit, full, text[...].astype(F32)).astype(BF16)


def _pairs(sizes, dest):
    return [
        (int(np.ravel_multi_index(at, sizes)), int(np.ravel_multi_index(dest(*at), sizes)))
        for at in np.ndindex(*sizes)
    ]


def shards(patches, ln_gain, ln_bias, merge_weight, merge_bias, targets, text_embed):
    sds = jax.ShapeDtypeStruct
    zl, xh, xl, yl, zh, c = (lax.axis_index(a) for a in ("zl", "xh", "xl", "yl", "zh", "c"))

    chunk = jnp.transpose(merge_weight, (2, 0, 1)).reshape(CHUNK, GROUP * FEAT)
    chunk = jnp.pad(chunk, ((0, CHUNK_PAD - CHUNK), (0, 0)))
    pair = jnp.stack([chunk, lax.ppermute(chunk, "xh", [(0, 1), (1, 0)])])
    pair_y = lax.ppermute(pair, "yl", [(0, 1), (1, 0)])
    packed = np.arange(4 * CHUNK)
    pack = np.zeros((4 * CHUNK, 4 * CHUNK_PAD), np.float32)
    pack[packed, packed // CHUNK * CHUNK_PAD + packed % CHUNK] = 1.0
    quad = _call(pack_body, sds((4 * CHUNK, GROUP * FEAT), BF16), 3, 1)(
        jnp.stack([xh, yl]).astype(jnp.int32), pair, pair_y, jnp.asarray(pack, BF16)
    )
    columns = lax.all_gather(quad, "yh")

    own, stats = _call(
        split_body,
        (sds((GROUP * FEAT, ROWS), BF16), sds((N_TP, 8, ROWS), F32)),
        1,
        scratch=[pltpu.VMEM((8, ROWS), F32)],
    )(patches)
    all_stats = lax.all_to_all(stats, TP, 0, 0, tiled=True)
    copies = pl.pallas_call(
        norm_body,
        out_shape=sds((4, GROUP * FEAT, ROWS), BF16),
        in_specs=_vmem(5),
        out_specs=pl.BlockSpec(memory_space=pltpu.HBM),
        scratch_shapes=[
            pltpu.VMEM((GROUP * FEAT, ROWS), BF16),
            pltpu.SemaphoreType.DMA((GROUP, 4)),
        ],
        compiler_params=pltpu.CompilerParams(vmem_limit_bytes=48 << 20),
    )(own, all_stats, ln_gain.astype(F32)[:, None], ln_bias.astype(F32)[:, None], pair_y)
    shared = lax.all_to_all(copies, SHARE, 0, 0, tiled=True)

    order = np.zeros((2, 4, FEAT, 4 * CHUNK), np.float32)
    for g in range(2):
        for r in range(FEAT):
            order[g, r // (2 * CHUNK), r, g * 2 * CHUNK + r % (2 * CHUNK)] = 1.0
    ids = jnp.stack([c, 2 * zl + xl]).astype(jnp.int32)
    piece = sds((4, FEAT, ROWS), BF16)
    send, keep = pl.pallas_call(
        project_body,
        out_shape=(piece, piece),
        in_specs=[pl.BlockSpec(memory_space=pltpu.SMEM)] + _vmem(3),
        out_specs=tuple(_vmem(2)),
        scratch_shapes=[pltpu.VMEM((2, FEAT, GROUP * FEAT), BF16)],
        compiler_params=pltpu.CompilerParams(vmem_limit_bytes=48 << 20),
    )(ids, shared, columns, jnp.asarray(order, BF16))

    got = lax.ppermute(send, "c", [(0, 1), (1, 0)])
    part = sds((FEAT, ROWS), BF16)
    parts = _call(pair_body, (part,) * 4, 2, 1)(zh[None].astype(jnp.int32), keep, got)
    axes, sizes = ("zl", "xl", "zh", "c"), (2, 2, 4, 2)
    moved = [
        lax.ppermute(
            parts[k],
            axes,
            _pairs(sizes, lambda z, x, h, k2, k=k: (z ^ k2, x ^ ((h ^ k) >> 1), 2 * z + ((h ^ k) & 1), x)),
        )
        for k in (2, 3, 1, 0)
    ]

    target_dev = targets // POS
    local_pos = targets % POS
    before = jnp.arange(ROWS)[:, None] < jnp.arange(ROWS)[None, :]
    rank = jnp.sum(((target_dev[:, None] == target_dev[None, :]) & before).astype(jnp.int32), axis=0)
    slot = (target_dev * SLOTS + rank)[None, :]
    zero = jnp.zeros((ROWS,), F32)
    one = jnp.ones((ROWS,), F32)
    tags = [(local_pos // 16 + 1).astype(F32), (local_pos % 16).astype(F32), one, zero, zero, zero, zero, zero]
    extra = jnp.stack(tags)

    sent = _call(place_body, sds((N_SEQ, SLOTS, LANES), BF16), 7)(
        *moved, merge_bias.astype(F32)[:, None], slot, extra
    )
    rows = lax.all_to_all(sent, SEQ, 0, 0, tiled=True)
    return _call(final_body, sds((FEAT, POS), BF16), 2)(rows, text_embed)


def solution(mesh):
    wide = Mesh(mesh.devices.reshape(2, 2, 2, 4, 2, 4, 2), ("zl", "xh", "xl", "yh", "yl", "zh", "c"))
    in_specs = (
        P(TP, SEQ),
        P(TP),
        P(TP),
        P(None, TP, SEQ),
        P(TP),
        P(SEQ),
        P(TP, SEQ),
    )
    return jax.shard_map(shards, mesh=wide, in_specs=in_specs, out_specs=P(TP, SEQ), check_vma=False)
```
